32 devices in a mesh: ctx: 16 (over z, x, core), head: 2 (over y).
Axes of the slice: x: 2, y: 2, z: 4, core: 2. Of those that a mesh axis runs over, the one named last changes fastest.
Arguments:
- queries: bfloat16 [4096, 64, 128], P(('ctx', 'head')), may hold values from -112 to 112
- key_heads: bfloat16 [4096, 8, 128], P(('ctx', 'head')), may hold values from -5 to 5
- head_values: bfloat16 [4096, 8, 128], P(('ctx', 'head')), may hold values from -6 to 6
- output_gradient: bfloat16 [4096, 64, 128], P(('ctx', 'head')), may hold values from -6 to 6
- doc_lengths: int32 [8], replicated, may hold values from 1 to 1024, 4096 in all
Outputs:
- attended: bfloat16 [4096, 64, 128], P(('ctx', 'head'))
- grad_queries: bfloat16 [4096, 64, 128], P(('ctx', 'head'))
- grad_keys: bfloat16 [4096, 8, 128], P(('ctx', 'head'))
- grad_values: bfloat16 [4096, 8, 128], P(('ctx', 'head'))
The draws below stay inside these ranges and needn't reach their ends.
Inputs may be any that keep to these rules, and one draw needn't show every extreme that they name: `doc_lengths`: the documents lie end to end and fill the sequence; the longest has exactly 1024 tokens.
All inputs are finite; a program needn't handle non-finite values.
Results may differ from the reference program's by a relative error of at most 0.0094.
Values may be sent and summed in bfloat16 or wider, within the bound.
A program may use at most 64 MiB of HBM per device.

```python
import math
import jax
import jax.numpy as jnp
import numpy as np
from jax import lax

QUERY_HEADS = 64
KEY_VALUE_HEADS = 8
HEAD_SIZE = 128
SHARD_TOKENS = 256
MOST = 1024
PACKED_TOKENS = 4096
DOCS = 8
STEPS = 4


def key_query_pair(key):
    key_sample = jnp.clip(jax.random.normal(jax.random.fold_in(key, 101), (PACKED_TOKENS, KEY_VALUE_HEADS, HEAD_SIZE), jnp.float32), -4.5, 4.5)
    query_draw = jnp.clip(jax.random.normal(jax.random.fold_in(key, 102), (PACKED_TOKENS, QUERY_HEADS, HEAD_SIZE), jnp.float32), -4.5, 4.5)
    return (key_sample, query_draw)


def draw_queries(key, part):
    return key_query_pair(key)[1].astype(jnp.bfloat16)


def draw_key_heads(key, part):
    return key_query_pair(key)[0].astype(jnp.bfloat16)


def level_of(rng, shape, split, smallest, largest):
    factor_of = 1.0
    for axis_at, shards_of in split:
        draws = jax.random.uniform(jax.random.fold_in(jax.random.fold_in(rng, 6), axis_at), (shards_of,), jnp.float32, smallest / len(split), largest / len(split))
        factor_of = factor_of * jnp.repeat(jnp.exp(draws), shape[axis_at] // shards_of).reshape((-1,) + (1,) * (len(shape) - 1 - axis_at))
    return factor_of


def profile(number_of, total, limit, skew):
    portions = [(1 << 20) // math.isqrt(rank ** skew) + 1 for rank in range(2, number_of + 1)]
    spare, given = total - limit - (number_of - 1), [1] * (number_of - 1)
    while spare > 0:
        candidates = [i for i in range(number_of - 1) if given[i] < limit]
        whole, remaining = sum([portions[i] for i in candidates]), spare
        for i in candidates:
            more = min(limit - given[i], max(1, remaining * portions[i] // whole), spare)
            given[i] = given[i] + more
            spare = spare - more
    return np.array([limit] + given)


def uneven(stream_key, count, total, limit, lean):
    if count == 2:
        one = jax.random.randint(stream_key, (), max(1, total - limit), min(limit, total - 1) + 1)
        return jnp.stack([one, total - one])
    tallies = jnp.asarray(profile(count, total, limit, lean), jnp.int32)
    couples = (count - 1) // 2
    donor, taker = tallies[1:1 + 2 * couples:2], tallies[2:2 + 2 * couples:2]
    margin = jnp.minimum(donor - 1, limit - taker)
    moved = jax.random.randint(jax.random.fold_in(stream_key, 1), (couples,), 0, 1 << 20) % (margin + 1)
    tallies = tallies.at[1:1 + 2 * couples:2].set(donor - moved).at[2:2 + 2 * couples:2].set(taker + moved)
    return tallies[jax.random.permutation(jax.random.fold_in(stream_key, 2), count)]


def gaussian(key, dims, deviation, most, cuts=(), kind=jnp.bfloat16):
    level = level_of(key, dims, cuts, -0.22, 0.18) if cuts else 1.0
    array = jax.random.normal(key, dims, jnp.float32) * deviation * level
    return jnp.minimum(jnp.maximum(array, -most), most).astype(kind)


def setup_inputs(seed: int = 0) -> dict:
    key_list = jax.random.split(jax.random.key(seed), 6)
    queries = draw_queries(jax.random.fold_in(key_list[5], 71), 0)
    key_heads = draw_key_heads(jax.random.fold_in(key_list[5], 71), 0)
    head_values = gaussian(key_list[2], (PACKED_TOKENS, KEY_VALUE_HEADS, HEAD_SIZE), 1.0, 6.0, ((0, 32),))
    output_gradient = gaussian(key_list[3], (PACKED_TOKENS, QUERY_HEADS, HEAD_SIZE), 1.0, 6.0, ((0, 32),))
    doc_lengths = uneven(key_list[4], DOCS, PACKED_TOKENS, MOST, 2).astype(jnp.int32)
    return dict(queries=queries, key_heads=key_heads, head_values=head_values, output_gradient=output_gradient, doc_lengths=doc_lengths)


def document_starts(doc_lengths, positions):
    doc_ends = jnp.cumsum(doc_lengths).astype(jnp.int32)
    earlier = jnp.where(doc_ends[None, :] <= positions[:, None], doc_lengths[None, :], 0)
    return jnp.sum(earlier, axis=1).astype(jnp.int32)


def reference(queries, key_heads, head_values, output_gradient, doc_lengths):
    query_group_width = QUERY_HEADS // KEY_VALUE_HEADS
    rows_in_window = STEPS * SHARD_TOKENS
    span_rows = rows_in_window + SHARD_TOKENS
    score_scale = HEAD_SIZE ** -0.5
    highest = lax.Precision.HIGHEST
    filler_rows = jnp.zeros((rows_in_window, KEY_VALUE_HEADS, HEAD_SIZE), jnp.bfloat16)
    padded_keys = jnp.concatenate([filler_rows, key_heads], 0)
    padded_values = jnp.concatenate([filler_rows, head_values], 0)
    positions = jnp.arange(PACKED_TOKENS, dtype=jnp.int32)
    starts = document_starts(doc_lengths, positions)

    def one_block(carry, block_index):
        key_sums, value_sums = carry
        leading_row = (block_index * SHARD_TOKENS).astype(jnp.int32)
        block_of_queries = lax.dynamic_slice_in_dim(queries, leading_row, SHARD_TOKENS, 0).astype(jnp.float32).reshape(SHARD_TOKENS, KEY_VALUE_HEADS, query_group_width, HEAD_SIZE)
        gradient_block = lax.dynamic_slice_in_dim(output_gradient, leading_row, SHARD_TOKENS, 0).astype(jnp.float32).reshape(SHARD_TOKENS, KEY_VALUE_HEADS, query_group_width, HEAD_SIZE)
        key_block = lax.dynamic_slice_in_dim(padded_keys, leading_row, span_rows, 0).astype(jnp.float32)
        value_block = lax.dynamic_slice_in_dim(padded_values, leading_row, span_rows, 0).astype(jnp.float32)
        query_pos = leading_row + jnp.arange(SHARD_TOKENS, dtype=jnp.int32)
        key_pos = leading_row - rows_in_window + jnp.arange(span_rows, dtype=jnp.int32)
        query_start = lax.dynamic_slice_in_dim(starts, leading_row, SHARD_TOKENS, 0)
        allowed = (key_pos[None, :] >= query_start[:, None]) & (key_pos[None, :] <= query_pos[:, None])
        scores = jnp.einsum("tkgd,skd->kgts", block_of_queries, key_block, precision=highest) * score_scale
        masked = jnp.where(allowed, scores, -jnp.inf)
        row_max = jnp.max(masked, axis=-1, keepdims=True)
        row_total = jnp.sum(jnp.exp(masked - row_max), axis=-1, keepdims=True)
        log_total = row_max + jnp.log(row_total)
        probabilities = jnp.where(allowed, jnp.exp(scores - log_total), 0.0)
        rounded = lax.optimization_barrier(probabilities.astype(jnp.bfloat16)).astype(jnp.float32)
        attended = jnp.einsum("kgts,skd->tkgd", rounded, value_block, precision=highest).astype(jnp.bfloat16)
        row_delta = jnp.sum(gradient_block * attended.astype(jnp.float32), axis=-1)
        row_delta = jnp.transpose(row_delta, (1, 2, 0))
        grad_weights = jnp.einsum("tkgd,skd->kgts", gradient_block, value_block, precision=highest)
        grad_scores = probabilities * (grad_weights - row_delta[..., None])
        grad_rounded = lax.optimization_barrier(grad_scores.astype(jnp.bfloat16)).astype(jnp.float32)
        grad_query = (score_scale * jnp.einsum("kgts,skd->tkgd", grad_rounded, key_block, precision=highest)).astype(jnp.bfloat16)
        key_part = score_scale * jnp.einsum("kgts,tkgd->skd", grad_rounded, block_of_queries, precision=highest)
        value_part = jnp.einsum("kgts,tkgd->skd", rounded, gradient_block, precision=highest)
        key_sums = lax.dynamic_update_slice_in_dim(key_sums, lax.dynamic_slice_in_dim(key_sums, leading_row, span_rows, 0) + key_part, leading_row, 0)
        value_sums = lax.dynamic_update_slice_in_dim(value_sums, lax.dynamic_slice_in_dim(value_sums, leading_row, span_rows, 0) + value_part, leading_row, 0)
        return (key_sums, value_sums), (attended, grad_query)

    blank_totals = jnp.zeros((PACKED_TOKENS + rows_in_window, KEY_VALUE_HEADS, HEAD_SIZE), jnp.float32)
    block_ids = jnp.arange(PACKED_TOKENS // SHARD_TOKENS, dtype=jnp.int32)
    (key_sums, value_sums), (attended, grad_query) = lax.scan(one_block, (blank_totals, blank_totals), block_ids)
    attended = attended.reshape(PACKED_TOKENS, QUERY_HEADS, HEAD_SIZE)
    grad_query = grad_query.reshape(PACKED_TOKENS, QUERY_HEADS, HEAD_SIZE)
    return attended, grad_query, key_sums[rows_in_window:].astype(jnp.bfloat16), value_sums[rows_in_window:].astype(jnp.bfloat16)
```

```python
import functools

import jax
import jax.numpy as jnp
from jax import lax
from jax.experimental import pallas as pl
from jax.experimental.pallas import tpu as pltpu
from jax.sharding import PartitionSpec as P

MOST = 1024
AXES = ("ctx", "head")
MASKED = -1e30


def document_starts(doc_lengths, positions):
    doc_ends = jnp.cumsum(doc_lengths)
    earlier = jnp.where(doc_ends[None, :] <= positions[:, None], doc_lengths[None, :], 0)
    return jnp.sum(earlier, axis=1)


def nt(left, right):
    return lax.dot_general(
        left, right, (((1,), (1,)), ((), ())), preferred_element_type=jnp.float32
    )


def nn(left, right):
    return jnp.dot(left, right, preferred_element_type=jnp.float32)


def attention_kernel(steps, rows, score_scale, *refs):
    bounds_ref, q_ref, do_ref = refs[:3]
    kv_refs = refs[3 : 4 + steps]
    o_ref, dq_ref = refs[4 + steps : 6 + steps]
    dkv_refs = refs[6 + steps : 7 + 2 * steps]
    bias, k_s, v_s, kt_s, vt_s, dk_s, dv_s = refs[7 + 2 * steps :]
    tokens, width, size_head = q_ref.shape
    span = (steps + 1) * tokens
    total_rows = tokens * width

    @pl.when(pl.program_id(0) == 0)
    def _():
        key_at = lax.broadcasted_iota(jnp.int32, (span, total_rows), 0)
        allowed = (key_at >= bounds_ref[0:1, :]) & (key_at <= bounds_ref[1:2, :])
        bias[...] = jnp.where(allowed, 0.0, MASKED)

    for i in range(steps + 1):
        at = pl.ds(i * tokens, tokens)
        k_s[at, :] = kv_refs[i][0]
        v_s[at, :] = kv_refs[i][1]
    kt_s[...] = k_s[...].T
    vt_s[...] = v_s[...].T
    dk_s[...] = jnp.zeros_like(dk_s)
    dv_s[...] = jnp.zeros_like(dv_s)
    part = rows // width

    @pl.loop(0, total_rows // rows)
    def _(c):
        toks = pl.ds(pl.multiple_of(c * part, part), part)
        lanes = pl.ds(pl.multiple_of(c * rows, rows), rows)
        q = q_ref[toks].reshape(rows, size_head)
        do = do_ref[toks].reshape(rows, size_head)
        x = nt(k_s[...], q) + bias[:, lanes]
        top = jnp.max(x, axis=0, keepdims=True)
        e = jnp.exp((x - top) * score_scale)
        inv = 1.0 / jnp.sum(e, axis=0, keepdims=True)
        p = e * inv
        w = p.astype(jnp.bfloat16)
        ot = nn(vt_s[...], w).astype(jnp.bfloat16)
        dot_f = do.T.astype(jnp.float32)
        delta = jnp.sum(dot_f * ot.astype(jnp.float32), axis=0, keepdims=True)
        o_ref[toks] = ot.T.reshape(part, width, size_head)
        dp = nt(v_s[...], do)
        ds = (p * (dp - delta)).astype(jnp.bfloat16)
        dv_s[...] += nn(w, do)
        dk_s[...] += nn(ds, q)
        dqt = (nn(kt_s[...], ds) * score_scale).astype(jnp.bfloat16)
        dq_ref[toks] = dqt.T.reshape(part, width, size_head)

    for i in range(steps + 1):
        at = pl.ds(i * tokens, tokens)
        dkv_refs[i][0] = (dk_s[at, :] * score_scale).astype(dkv_refs[i].dtype)
        dkv_refs[i][1] = dv_s[at, :].astype(dkv_refs[i].dtype)


def attention(queries, output_gradient, kv_blocks, bounds, score_scale):
    tokens, heads, size_head = queries.shape
    kv_count = kv_blocks[0].shape[1]
    width = heads // kv_count
    steps = len(kv_blocks) - 1
    span = (steps + 1) * tokens
    total_rows = tokens * width
    rows = min(256, total_rows)
    q4 = queries.reshape(tokens, kv_count, width, size_head)
    do4 = output_gradient.reshape(tokens, kv_count, width, size_head)
    row_spec = pl.BlockSpec((tokens, None, width, size_head), lambda g: (0, g, 0, 0))
    kv_spec = pl.BlockSpec((2, None, tokens, size_head), lambda g: (0, g, 0, 0))
    row_shape = jax.ShapeDtypeStruct(q4.shape, jnp.bfloat16)
    sent = jax.ShapeDtypeStruct(kv_blocks[0].shape, jnp.bfloat16)
    kept = jax.ShapeDtypeStruct(kv_blocks[0].shape, jnp.float32)
    outs = pl.pallas_call(
        functools.partial(attention_kernel, steps, rows, score_scale),
        grid=(kv_count,),
        in_specs=[pl.BlockSpec((2, total_rows), lambda g: (0, 0)), row_spec, row_spec]
        + [kv_spec] * (steps + 1),
        out_specs=[row_spec, row_spec] + [kv_spec] * (steps + 1),
        out_shape=[row_shape, row_shape] + [sent] * steps + [kept],
        scratch_shapes=[
            pltpu.VMEM((span, total_rows), jnp.float32),
            pltpu.VMEM((span, size_head), jnp.bfloat16),
            pltpu.VMEM((span, size_head), jnp.bfloat16),
            pltpu.VMEM((size_head, span), jnp.bfloat16),
            pltpu.VMEM((size_head, span), jnp.bfloat16),
            pltpu.VMEM((span, size_head), jnp.float32),
            pltpu.VMEM((span, size_head), jnp.float32),
        ],
        compiler_params=pltpu.CompilerParams(
            dimension_semantics=("arbitrary",), vmem_limit_bytes=56 << 20
        ),
        name="attention",
    )(bounds, q4, do4, *kv_blocks)
    return outs[0].reshape(queries.shape), outs[1].reshape(queries.shape), outs[2:]


def body(queries, key_heads, head_values, output_gradient, doc_lengths):
    tokens, heads, size_head = queries.shape
    width = heads // key_heads.shape[1]
    devices = lax.axis_size("ctx") * lax.axis_size("head")
    steps = (MOST + tokens - 2) // tokens
    base = (lax.axis_index("ctx") * lax.axis_size("head") + lax.axis_index("head")) * tokens
    query_pos = base + jnp.arange(tokens, dtype=jnp.int32)
    query_start = document_starts(doc_lengths, query_pos)
    window_base = base - steps * tokens
    bounds = jnp.stack([query_start, query_pos], 0) - window_base
    bounds = jnp.repeat(bounds, width, axis=1)

    own = jnp.transpose(jnp.stack([key_heads, head_values], 0), (0, 2, 1, 3))

    def moved(block, distance):
        route = [(i, (i + distance) % devices) for i in range(devices)]
        return lax.ppermute(block, AXES, route)

    blocks = [moved(own, s) for s in range(steps, 0, -1)] + [own]
    attended, grad_query, parts = attention(
        queries, output_gradient, blocks, bounds, size_head ** (-0.5)
    )
    total = parts[steps]
    for i in range(steps):
        total = total + moved(parts[i], i - steps).astype(jnp.float32)
    total = jnp.transpose(total.astype(jnp.bfloat16), (0, 2, 1, 3))
    return attended, grad_query, total[0], total[1]


def solution(mesh):
    whole = P(AXES, None, None)
    return jax.shard_map(
        body,
        mesh=mesh,
        in_specs=(whole, whole, whole, whole, P()),
        out_specs=(whole, whole, whole, whole),
        check_vma=False,
    )
```

```python
import functools

import jax
import jax.numpy as jnp
from jax import lax
from jax.experimental import pallas as pl
from jax.experimental.pallas import tpu as pltpu
from jax.sharding import PartitionSpec as P

MOST = 1024
AXES = ("ctx", "head")
MASKED = -1e30


def document_starts(doc_lengths, positions):
    doc_ends = jnp.cumsum(doc_lengths)
    earlier = jnp.where(doc_ends[None, :] <= positions[:, None], doc_lengths[None, :], 0)
    return jnp.sum(earlier, axis=1)


def nt(left, right):
    return lax.dot_general(
        left, right, (((1,), (1,)), ((), ())), preferred_element_type=jnp.float32
    )


def nn(left, right):
    return jnp.dot(left, right, preferred_element_type=jnp.float32)


def attention_kernel(
    steps, rows, ctx_size, head_size, ahead, behind, score_scale,
    bounds_ref, q_ref, do_ref, own_ref, o_ref, dq_ref, dkv_ref,
    window, leaving, landed, own_part, bias, k_s, v_s, kt_s, vt_s, dk_s, dv_s,
    kv_send, kv_recv, d_send, d_recv,
):
    tokens, width, size_head = q_ref.shape
    span = (steps + 1) * tokens
    total_rows = tokens * width
    devices = ctx_size * head_size
    g = pl.program_id(0)
    kv_count = pl.num_programs(0)
    me = lax.axis_index("ctx") * head_size + lax.axis_index("head")

    def peer(distance):
        other = lax.rem(me + distance + devices, devices)
        return (other // head_size, lax.rem(other, head_size))

    def send_block(head, s):
        return pltpu.make_async_remote_copy(
            src_ref=own_ref.at[head],
            dst_ref=window.at[head, steps - s],
            send_sem=kv_send.at[head],
            recv_sem=kv_recv.at[head],
            device_id=peer(s),
            device_id_type=pl.DeviceIdType.MESH,
        )

    def send_part(head, s):
        return pltpu.make_async_remote_copy(
            src_ref=leaving.at[head, steps - s],
            dst_ref=landed.at[head, steps - s],
            send_sem=d_send.at[head],
            recv_sem=d_recv.at[head],
            device_id=peer(-s),
            device_id_type=pl.DeviceIdType.MESH,
        )

    def send_blocks(head):
        @pl.loop(0, steps)
        def _(i):
            send_block(head, steps - i).start()

    def send_parts(head):
        @pl.loop(0, steps)
        def _(i):
            send_part(head, steps - i).start()

    def wait_all(ref, sem):
        pltpu.make_async_copy(ref, ref, sem).wait()

    def finish(head):
        wait_all(landed.at[head], d_recv.at[head])
        for which in range(2):
            total = own_part[head, which]
            for i in range(steps):
                total = total + landed[head, i, which].astype(jnp.float32)
            dkv_ref[head, which] = total.astype(dkv_ref.dtype)

    @pl.when(g == 0)
    def _():
        barrier = pltpu.get_barrier_semaphore()

        @pl.loop(1, steps + 1)
        def _(s):
            for d in (s, -s):
                pl.semaphore_signal(
                    barrier, inc=1, device_id=peer(d), device_id_type=pl.DeviceIdType.MESH
                )

        pl.semaphore_wait(barrier, 2 * steps)

        @pl.loop(0, ahead)
        def _(head):
            send_blocks(head)

        key_at = lax.broadcasted_iota(jnp.int32, (span, total_rows), 0)
        allowed = (key_at >= bounds_ref[0:1, :]) & (key_at <= bounds_ref[1:2, :])
        bias[...] = jnp.where(allowed, 0.0, MASKED)

    @pl.when(g + ahead < kv_count)
    def _():
        send_blocks(g + ahead)

    @pl.when(g > 0)
    def _():
        send_parts(g - 1)

    wait_all(window.at[g], kv_recv.at[g])
    for i in range(steps + 1):
        at = pl.ds(i * tokens, tokens)
        k_s[at, :] = window[g, i, 0] if i < steps else own_ref[g, 0]
        v_s[at, :] = window[g, i, 1] if i < steps else own_ref[g, 1]
    kt_s[...] = k_s[...].T
    vt_s[...] = v_s[...].T
    dk_s[...] = jnp.zeros_like(dk_s)
    dv_s[...] = jnp.zeros_like(dv_s)
    part = rows // width

    @pl.loop(0, total_rows // rows)
    def _(c):
        toks = pl.ds(pl.multiple_of(c * part, part), part)
        lanes = pl.ds(pl.multiple_of(c * rows, rows), rows)
        q = q_ref[toks].reshape(rows, size_head)
        do = do_ref[toks].reshape(rows, size_head)
        x = nt(k_s[...], q) + bias[:, lanes]
        top = jnp.max(x, axis=0, keepdims=True)
        e = jnp.exp((x - top) * score_scale)
        inv = 1.0 / jnp.sum(e, axis=0, keepdims=True)
        p = e * inv
        w = p.astype(jnp.bfloat16)
        ot = nn(vt_s[...], w).astype(jnp.bfloat16)
        dot_f = do.T.astype(jnp.float32)
        delta = jnp.sum(dot_f * ot.astype(jnp.float32), axis=0, keepdims=True)
        o_ref[toks] = ot.T.reshape(part, width, size_head)
        dp = nt(v_s[...], do)
        ds = (p * (dp - delta)).astype(jnp.bfloat16)
        dv_s[...] += nn(w, do)
        dk_s[...] += nn(ds, q)
        dqt = (nn(kt_s[...], ds) * score_scale).astype(jnp.bfloat16)
        dq_ref[toks] = dqt.T.reshape(part, width, size_head)

    for i in range(steps):
        at = pl.ds(i * tokens, tokens)
        leaving[g, i, 0] = (dk_s[at, :] * score_scale).astype(leaving.dtype)
        leaving[g, i, 1] = dv_s[at, :].astype(leaving.dtype)
    at = pl.ds(steps * tokens, tokens)
    own_part[g, 0] = dk_s[at, :] * score_scale
    own_part[g, 1] = dv_s[at, :]

    @pl.when(g >= behind)
    def _():
        finish(g - behind)

    @pl.when(g == kv_count - 1)
    def _():
        send_parts(g)

        @pl.loop(0, behind)
        def _(i):
            finish(g - behind + 1 + i)

        @pl.loop(0, kv_count)
        def _(head):
            wait_all(window.at[head], kv_send.at[head])
            wait_all(leaving.at[head], d_send.at[head])


def attention(queries, output_gradient, own, bounds, steps, score_scale):
    tokens, heads, size_head = queries.shape
    kv_count = own.shape[0]
    width = heads // kv_count
    span = (steps + 1) * tokens
    total_rows = tokens * width
    rows = min(256, total_rows)
    q4 = queries.reshape(tokens, kv_count, width, size_head)
    do4 = output_gradient.reshape(tokens, kv_count, width, size_head)
    row_spec = pl.BlockSpec((tokens, None, width, size_head), lambda g: (0, g, 0, 0))
    row_shape = jax.ShapeDtypeStruct(q4.shape, jnp.bfloat16)
    full = pl.BlockSpec(own.shape, lambda g: (0, 0, 0, 0))
    slots = (kv_count, steps) + own.shape[1:]
    outs = pl.pallas_call(
        functools.partial(
            attention_kernel,
            steps,
            rows,
            lax.axis_size("ctx"),
            lax.axis_size("head"),
            min(3, kv_count),
            min(3, kv_count - 1),
            score_scale,
        ),
        grid=(kv_count,),
        in_specs=[pl.BlockSpec((2, total_rows), lambda g: (0, 0)), row_spec, row_spec, full],
        out_specs=[row_spec, row_spec, full],
        out_shape=[row_shape, row_shape, jax.ShapeDtypeStruct(own.shape, jnp.bfloat16)],
        scratch_shapes=[
            pltpu.VMEM(slots, jnp.bfloat16),
            pltpu.VMEM(slots, jnp.bfloat16),
            pltpu.VMEM(slots, jnp.bfloat16),
            pltpu.VMEM(own.shape, jnp.float32),
            pltpu.VMEM((span, total_rows), jnp.float32),
            pltpu.VMEM((span, size_head), jnp.bfloat16),
            pltpu.VMEM((span, size_head), jnp.bfloat16),
            pltpu.VMEM((size_head, span), jnp.bfloat16),
            pltpu.VMEM((size_head, span), jnp.bfloat16),
            pltpu.VMEM((span, size_head), jnp.float32),
            pltpu.VMEM((span, size_head), jnp.float32),
            pltpu.SemaphoreType.DMA((kv_count,)),
            pltpu.SemaphoreType.DMA((kv_count,)),
            pltpu.SemaphoreType.DMA((kv_count,)),
            pltpu.SemaphoreType.DMA((kv_count,)),
        ],
        compiler_params=pltpu.CompilerParams(
            dimension_semantics=("arbitrary",),
            vmem_limit_bytes=60 << 20,
            collective_id=0,
            has_side_effects=True,
        ),
        name="attention",
    )(bounds, q4, do4, own)
    return outs[0].reshape(queries.shape), outs[1].reshape(queries.shape), outs[2]


def body(queries, key_heads, head_values, output_gradient, doc_lengths):
    tokens, heads, size_head = queries.shape
    width = heads // key_heads.shape[1]
    steps = (MOST + tokens - 2) // tokens
    base = (lax.axis_index("ctx") * lax.axis_size("head") + lax.axis_index("head")) * tokens
    query_pos = base + jnp.arange(tokens, dtype=jnp.int32)
    query_start = document_starts(doc_lengths, query_pos)
    window_base = base - steps * tokens
    bounds = jnp.stack([query_start, query_pos], 0) - window_base
    bounds = jnp.repeat(bounds, width, axis=1)
    own = jnp.transpose(jnp.stack([key_heads, head_values], 0), (2, 0, 1, 3))
    attended, grad_query, total = attention(
        queries, output_gradient, own, bounds, steps, size_head ** (-0.5)
    )
    total = jnp.transpose(total, (1, 2, 0, 3))
    return attended, grad_query, total[0], total[1]


def solution(mesh):
    whole = P(AXES, None, None)
    return jax.shard_map(
        body,
        mesh=mesh,
        in_specs=(whole, whole, whole, whole, P()),
        out_specs=(whole, whole, whole, whole),
        check_vma=False,
    )
```

```python
import functools

import jax
import jax.numpy as jnp
from jax import lax
from jax.experimental import pallas as pl
from jax.experimental.pallas import tpu as pltpu
from jax.sharding import PartitionSpec as P

MOST = 1024
AXES = ("ctx", "head")
MASKED = -1e30


def document_starts(doc_lengths, positions):
    doc_ends = jnp.cumsum(doc_lengths)
    earlier = jnp.where(doc_ends[None, :] <= positions[:, None], doc_lengths[None, :], 0)
    return jnp.sum(earlier, axis=1)


def nt(left, right):
    return lax.dot_general(
        left, right, (((1,), (1,)), ((), ())), preferred_element_type=jnp.float32
    )


def nn(left, right):
    return jnp.dot(left, right, preferred_element_type=jnp.float32)


def attention_kernel(
    steps, rows, ctx_size, head_size, ahead, behind, score_scale,
    bounds_ref, q_ref, do_ref, own_ref, o_ref, dq_ref, dkv_ref,
    window, leaving, landed, own_part, bias, q_s, do_s, o_s, dq_s,
    k_s, v_s, kt_s, vt_s, dk_s, dv_s,
    kv_send, kv_recv, d_send, d_recv, row_here, row_send, row_recv, out_here, out_send, out_recv,
):
    local_heads, slots = window.shape[:2]
    tokens, width, size_head = q_s.shape[2:]
    span = (steps + 1) * tokens
    total_rows = tokens * width
    part = rows // width
    g = pl.program_id(0)
    ctx = lax.axis_index("ctx")
    core = lax.rem(ctx, 2)
    me = ctx * head_size + lax.axis_index("head")
    base = me - core * head_size
    devices = ctx_size * head_size
    mesh_ids = pl.DeviceIdType.MESH
    sibling = (ctx + 1 - 2 * core, lax.axis_index("head"))

    def at_device(flat):
        return (flat // head_size, lax.rem(flat, head_size))

    def each_target(visit):
        @pl.loop(0, slots)
        def _(i):
            chip = me - head_size + i

            @pl.when((chip >= 0) & (chip < devices))
            def _():
                @pl.when(lax.rem(chip // head_size, 2) == 0)
                def _():
                    for side in range(2):
                        target = chip + side * head_size

                        @pl.when(target != me)
                        def _():
                            visit(i, side, target)

    def each_source(visit):
        @pl.loop(0, slots)
        def _(j):
            source = base - steps + j

            @pl.when((source >= 0) & (source != me))
            def _():
                visit(j, source)

    def block_copy(k, i, side, target):
        slot = slots - 1 - i
        return pltpu.make_async_remote_copy(
            src_ref=own_ref.at[side * local_heads + k],
            dst_ref=window.at[k, slot],
            send_sem=kv_send.at[k],
            recv_sem=kv_recv.at[k, slot],
            device_id=at_device(target),
            device_id_type=mesh_ids,
        )

    def part_copy(k, j, source):
        head = core * local_heads + k
        return pltpu.make_async_remote_copy(
            src_ref=leaving.at[k, j],
            dst_ref=landed.at[head, slots - 1 - j],
            send_sem=d_send.at[k],
            recv_sem=d_recv.at[head, slots - 1 - j],
            device_id=at_device(source),
            device_id_type=mesh_ids,
        )

    def row_copies(k, n):
        src, dst = ((q_ref, q_s), (do_ref, do_s))[n]
        here = pltpu.make_async_copy(
            src.at[:, core * local_heads + k], dst.at[k, core], row_here.at[k, n]
        )
        away = pltpu.make_async_remote_copy(
            src_ref=src.at[:, (1 - core) * local_heads + k],
            dst_ref=dst.at[k, core],
            send_sem=row_send.at[k, n],
            recv_sem=row_recv.at[k, n],
            device_id=sibling,
            device_id_type=mesh_ids,
        )
        return here, away

    def out_copies(k, n):
        src, dst = ((o_s, o_ref), (dq_s, dq_ref))[n]
        head = core * local_heads + k
        here = pltpu.make_async_copy(src.at[k, core], dst.at[:, head], out_here.at[k, n])
        away = pltpu.make_async_remote_copy(
            src_ref=src.at[k, 1 - core],
            dst_ref=dst.at[:, head],
            send_sem=out_send.at[k, n],
            recv_sem=out_recv.at[k, n],
            device_id=sibling,
            device_id_type=mesh_ids,
        )
        return here, away

    def fetch(k):
        for n in range(2):
            here, away = row_copies(k, n)
            away.start()
            here.start()
        each_target(lambda i, side, target: block_copy(k, i, side, target).start())

    def give(k):
        each_source(lambda j, source: part_copy(k, j, source).start())
        for n in range(2):
            here, away = out_copies(k, n)
            away.start()
            here.start()

    def finish(k):
        def add(i, side, target):
            head = side * local_heads + k
            pltpu.make_async_copy(landed.at[head, i], landed.at[head, i], d_recv.at[head, i]).wait()
            own_part[head] += landed[head, i].astype(jnp.float32)

        each_target(add)
        for side in range(2):
            head = side * local_heads + k
            dkv_ref[head] = own_part[head].astype(dkv_ref.dtype)

    @pl.when(g == 0)
    def _():
        barrier = pltpu.get_barrier_semaphore()

        def greet(flat):
            pl.semaphore_signal(
                barrier, inc=1, device_id=at_device(flat), device_id_type=mesh_ids
            )

        each_target(lambda i, side, target: greet(target))
        each_source(lambda j, source: greet(source))
        greeted = jnp.int32(0)
        for i in range(slots):
            chip = me - head_size + i
            is_chip = (chip >= 0) & (chip < devices)
            is_chip = is_chip & (lax.rem(chip // head_size, 2) == 0)
            for side in range(2):
                met = is_chip & (chip + side * head_size != me)
                greeted = greeted + jnp.where(met, 1, 0)
            source = base - steps + i
            greeted = greeted + jnp.where((source >= 0) & (source != me), 1, 0)
        pl.semaphore_wait(barrier, greeted)

        @pl.loop(0, ahead)
        def _(k):
            fetch(k)

        own_part[...] = jnp.zeros_like(own_part)
        key_at = lax.broadcasted_iota(jnp.int32, (span, total_rows), 0)
        for b in range(2):
            low, high = bounds_ref[2 * b : 2 * b + 1, :], bounds_ref[2 * b + 1 : 2 * b + 2, :]
            bias[b] = jnp.where((key_at >= low) & (key_at <= high), 0.0, MASKED)

    @pl.when((g > 0) & (g + ahead - 1 < local_heads))
    def _():
        fetch(g + ahead - 1)

    @pl.when(g > 0)
    def _():
        give(g - 1)

    for n in range(2):
        here, away = row_copies(g, n)
        here.wait()
        away.wait_recv()

    @pl.loop(0, slots)
    def _(j):
        source = base - steps + j
        at = pl.ds(pl.multiple_of(j * tokens, tokens), tokens)

        @pl.when(source < 0)
        def _():
            k_s[at, :] = jnp.zeros((tokens, size_head), k_s.dtype)
            v_s[at, :] = jnp.zeros((tokens, size_head), v_s.dtype)

        @pl.when(source == me)
        def _():
            k_s[at, :] = own_ref[core * local_heads + g, 0]
            v_s[at, :] = own_ref[core * local_heads + g, 1]

        @pl.when((source >= 0) & (source != me))
        def _():
            pltpu.make_async_copy(window.at[g, j], window.at[g, j], kv_recv.at[g, j]).wait()
            k_s[at, :] = window[g, j, 0]
            v_s[at, :] = window[g, j, 1]

    kt_s[...] = k_s[...].T
    vt_s[...] = v_s[...].T
    dk_s[...] = jnp.zeros_like(dk_s)
    dv_s[...] = jnp.zeros_like(dv_s)

    for b in range(2):
        near = pl.ds(b * head_size * tokens, span)

        @pl.loop(0, total_rows // rows)
        def _(c):
            toks = pl.ds(pl.multiple_of(c * part, part), part)
            lanes = pl.ds(pl.multiple_of(c * rows, rows), rows)
            q = q_s[g, b, toks].reshape(rows, size_head)
            do = do_s[g, b, toks].reshape(rows, size_head)
            x = nt(k_s[near, :], q) + bias[b, :, lanes]
            top = jnp.max(x, axis=0, keepdims=True)
            e = jnp.exp((x - top) * score_scale)
            inv = 1.0 / jnp.sum(e, axis=0, keepdims=True)
            p = e * inv
            w = p.astype(jnp.bfloat16)
            ot = nn(vt_s[:, near], w).astype(jnp.bfloat16)
            dot_f = do.T.astype(jnp.float32)
            delta = jnp.sum(dot_f * ot.astype(jnp.float32), axis=0, keepdims=True)
            o_s[g, b, toks] = ot.T.reshape(part, width, size_head)
            dp = nt(v_s[near, :], do)
            ds = (p * (dp - delta)).astype(jnp.bfloat16)
            dv_s[near, :] += nn(w, do)
            dk_s[near, :] += nn(ds, q)
            dqt = (nn(kt_s[:, near], ds) * score_scale).astype(jnp.bfloat16)
            dq_s[g, b, toks] = dqt.T.reshape(part, width, size_head)

    for j in range(slots):
        at = pl.ds(j * tokens, tokens)
        leaving[g, j, 0] = (dk_s[at, :] * score_scale).astype(leaving.dtype)
        leaving[g, j, 1] = dv_s[at, :].astype(leaving.dtype)
    at = pl.ds(pl.multiple_of((steps + core * head_size) * tokens, tokens), tokens)
    own_part[core * local_heads + g, 0] += dk_s[at, :] * score_scale
    own_part[core * local_heads + g, 1] += dv_s[at, :]

    @pl.when(g >= behind)
    def _():
        finish(g - behind)

    @pl.when(g == local_heads - 1)
    def _():
        give(g)

        @pl.loop(0, behind)
        def _(i):
            finish(g - behind + 1 + i)

        @pl.loop(0, local_heads)
        def _(k):
            each_target(lambda i, side, target: block_copy(k, i, side, target).wait_send())
            each_source(lambda j, source: part_copy(k, j, source).wait_send())
            for n in range(2):
                row_copies(k, n)[1].wait_send()
                here, away = out_copies(k, n)
                here.wait()
                away.wait()


def attention(queries, output_gradient, own, bounds, steps, score_scale):
    tokens, heads, size_head = queries.shape
    kv_count = own.shape[0]
    width = heads // kv_count
    local_heads = kv_count // 2
    span = (steps + 1) * tokens
    slots = steps + 1 + lax.axis_size("head")
    reach = slots * tokens
    total_rows = tokens * width
    rows = min(256, total_rows)
    q4 = queries.reshape(tokens, kv_count, width, size_head)
    do4 = output_gradient.reshape(tokens, kv_count, width, size_head)
    anywhere = pl.BlockSpec(memory_space=pl.ANY)
    row_shape = jax.ShapeDtypeStruct(q4.shape, jnp.bfloat16)
    full = pl.BlockSpec(own.shape, lambda g: (0, 0, 0, 0))
    row_buffer = pltpu.VMEM((local_heads, 2, tokens, width, size_head), jnp.bfloat16)
    pair = pltpu.SemaphoreType.DMA((local_heads, 2))
    outs = pl.pallas_call(
        functools.partial(
            attention_kernel,
            steps,
            rows,
            lax.axis_size("ctx"),
            lax.axis_size("head"),
            min(2, local_heads),
            min(2, local_heads - 1),
            score_scale,
        ),
        grid=(local_heads,),
        in_specs=[pl.BlockSpec((4, total_rows), lambda g: (0, 0)), anywhere, anywhere, full],
        out_specs=[anywhere, anywhere, full],
        out_shape=[row_shape, row_shape, jax.ShapeDtypeStruct(own.shape, jnp.bfloat16)],
        scratch_shapes=[
            pltpu.VMEM((local_heads, slots) + own.shape[1:], jnp.bfloat16),
            pltpu.VMEM((local_heads, slots) + own.shape[1:], jnp.bfloat16),
            pltpu.VMEM((kv_count, slots) + own.shape[1:], jnp.bfloat16),
            pltpu.VMEM(own.shape, jnp.float32),
            pltpu.VMEM((2, span, total_rows), jnp.float32),
            row_buffer,
            row_buffer,
            row_buffer,
            row_buffer,
            pltpu.VMEM((reach, size_head), jnp.bfloat16),
            pltpu.VMEM((reach, size_head), jnp.bfloat16),
            pltpu.VMEM((size_head, reach), jnp.bfloat16),
            pltpu.VMEM((size_head, reach), jnp.bfloat16),
            pltpu.VMEM((reach, size_head), jnp.float32),
            pltpu.VMEM((reach, size_head), jnp.float32),
            pltpu.SemaphoreType.DMA((local_heads,)),
            pltpu.SemaphoreType.DMA((local_heads, slots)),
            pltpu.SemaphoreType.DMA((local_heads,)),
            pltpu.SemaphoreType.DMA((kv_count, slots)),
            pair,
            pair,
            pair,
            pair,
            pair,
            pair,
        ],
        compiler_params=pltpu.CompilerParams(
            dimension_semantics=("arbitrary",),
            vmem_limit_bytes=60 << 20,
            collective_id=0,
            has_side_effects=True,
        ),
        name="attention",
    )(bounds, q4, do4, own)
    return outs[0].reshape(queries.shape), outs[1].reshape(queries.shape), outs[2]


def body(queries, key_heads, head_values, output_gradient, doc_lengths):
    tokens, heads, size_head = queries.shape
    width = heads // key_heads.shape[1]
    steps = (MOST + tokens - 2) // tokens
    ctx, head_size = lax.axis_index("ctx"), lax.axis_size("head")
    chip = (ctx - ctx % 2) * head_size + lax.axis_index("head")
    within = jnp.arange(tokens, dtype=jnp.int32)
    bounds = []
    for b in range(2):
        base = (chip + b * head_size) * tokens
        window_base = base - steps * tokens
        query_pos = base + within
        bounds += [document_starts(doc_lengths, query_pos) - window_base, query_pos - window_base]
    bounds = jnp.repeat(jnp.stack(bounds, 0), width, axis=1)
    own = jnp.transpose(jnp.stack([key_heads, head_values], 0), (2, 0, 1, 3))
    attended, grad_query, total = attention(
        queries, output_gradient, own, bounds, steps, size_head ** (-0.5)
    )
    total = jnp.transpose(total, (1, 2, 0, 3))
    return attended, grad_query, total[0], total[1]


def solution(mesh):
    whole = P(AXES, None, None)
    return jax.shard_map(
        body,
        mesh=mesh,
        in_specs=(whole, whole, whole, whole, P()),
        out_specs=(whole, whole, whole, whole),
        check_vma=False,
    )
```

```python
import functools

import jax
import jax.numpy as jnp
from jax import lax
from jax.experimental import pallas as pl
from jax.experimental.pallas import tpu as pltpu
from jax.sharding import PartitionSpec as P

MOST = 1024
AXES = ("ctx", "head")
MASKED = -1e30


def document_starts(doc_lengths, positions):
    doc_ends = jnp.cumsum(doc_lengths)
    earlier = jnp.where(doc_ends[None, :] <= positions[:, None], doc_lengths[None, :], 0)
    return jnp.sum(earlier, axis=1)


def nt(left, right):
    return lax.dot_general(
        left, right, (((1,), (1,)), ((), ())), preferred_element_type=jnp.float32
    )


def nn(left, right):
    return jnp.dot(left, right, preferred_element_type=jnp.float32)


def attention_kernel(
    steps, rows, ctx_size, head_size, ahead, behind, score_scale,
    bounds_ref, q_ref, do_ref, own_ref, o_ref, dq_ref, dk_ref, dv_ref,
    window, leaving, landed, own_part, bias, q_s, do_s, o_s, dq_s,
    k_s, v_s, kt_s, vt_s, dk_s, dv_s,
    kv_send, kv_recv, d_send, d_recv, row_here, row_send, row_recv, out_here, out_send, out_recv,
):
    local_heads, slots = window.shape[:2]
    tokens, width, size_head = q_s.shape[2:]
    span = (steps + 1) * tokens
    total_rows = tokens * width
    part = rows // width
    g = pl.program_id(0)
    ctx = lax.axis_index("ctx")
    core = lax.rem(ctx, 2)
    me = ctx * head_size + lax.axis_index("head")
    base = me - core * head_size
    devices = ctx_size * head_size
    mesh_ids = pl.DeviceIdType.MESH
    sibling = (ctx + 1 - 2 * core, lax.axis_index("head"))

    def at_device(flat):
        return (flat // head_size, lax.rem(flat, head_size))

    def each_target(visit):
        @pl.loop(0, slots)
        def _(i):
            chip = me - head_size + i

            @pl.when((chip >= 0) & (chip < devices))
            def _():
                @pl.when(lax.rem(chip // head_size, 2) == 0)
                def _():
                    for side in range(2):
                        target = chip + side * head_size

                        @pl.when(target != me)
                        def _():
                            visit(i, side, target)

    def each_source(visit):
        @pl.loop(0, slots)
        def _(j):
            source = base - steps + j

            @pl.when((source >= 0) & (source != me))
            def _():
                visit(j, source)

    def block_copy(k, i, side, target):
        slot = slots - 1 - i
        return pltpu.make_async_remote_copy(
            src_ref=own_ref.at[side * local_heads + k],
            dst_ref=window.at[k, slot],
            send_sem=kv_send.at[k],
            recv_sem=kv_recv.at[k, slot],
            device_id=at_device(target),
            device_id_type=mesh_ids,
        )

    def part_copy(k, j, source):
        head = core * local_heads + k
        return pltpu.make_async_remote_copy(
            src_ref=leaving.at[k, j],
            dst_ref=landed.at[head, slots - 1 - j],
            send_sem=d_send.at[k],
            recv_sem=d_recv.at[head, slots - 1 - j],
            device_id=at_device(source),
            device_id_type=mesh_ids,
        )

    def row_copies(k, n):
        src, dst = ((q_ref, q_s), (do_ref, do_s))[n]
        here = pltpu.make_async_copy(
            src.at[:, core * local_heads + k], dst.at[k, core], row_here.at[k, n]
        )
        away = pltpu.make_async_remote_copy(
            src_ref=src.at[:, (1 - core) * local_heads + k],
            dst_ref=dst.at[k, core],
            send_sem=row_send.at[k, n],
            recv_sem=row_recv.at[k, n],
            device_id=sibling,
            device_id_type=mesh_ids,
        )
        return here, away

    def out_copies(k, n):
        src, dst = ((o_s, o_ref), (dq_s, dq_ref))[n]
        head = core * local_heads + k
        here = pltpu.make_async_copy(src.at[k, core], dst.at[:, head], out_here.at[k, n])
        away = pltpu.make_async_remote_copy(
            src_ref=src.at[k, 1 - core],
            dst_ref=dst.at[:, head],
            send_sem=out_send.at[k, n],
            recv_sem=out_recv.at[k, n],
            device_id=sibling,
            device_id_type=mesh_ids,
        )
        return here, away

    def fetch(k):
        for n in range(2):
            here, away = row_copies(k, n)
            away.start()
            here.start()
        each_target(lambda i, side, target: block_copy(k, i, side, target).start())

    def give(k):
        each_source(lambda j, source: part_copy(k, j, source).start())
        for n in range(2):
            here, away = out_copies(k, n)
            away.start()
            here.start()

    def finish(k):
        def add(i, side, target):
            head = side * local_heads + k
            pltpu.make_async_copy(landed.at[head, i], landed.at[head, i], d_recv.at[head, i]).wait()
            own_part[head] += landed[head, i].astype(jnp.float32)

        each_target(add)
        for side in range(2):
            head = side * local_heads + k
            dk_ref[head] = own_part[head, 0].astype(dk_ref.dtype)
            dv_ref[head] = own_part[head, 1].astype(dv_ref.dtype)

    @pl.when(g == 0)
    def _():
        barrier = pltpu.get_barrier_semaphore()

        def greet(flat):
            pl.semaphore_signal(
                barrier, inc=1, device_id=at_device(flat), device_id_type=mesh_ids
            )

        each_target(lambda i, side, target: greet(target))
        each_source(lambda j, source: greet(source))
        greeted = jnp.int32(0)
        for i in range(slots):
            chip = me - head_size + i
            is_chip = (chip >= 0) & (chip < devices)
            is_chip = is_chip & (lax.rem(chip // head_size, 2) == 0)
            for side in range(2):
                met = is_chip & (chip + side * head_size != me)
                greeted = greeted + jnp.where(met, 1, 0)
            source = base - steps + i
            greeted = greeted + jnp.where((source >= 0) & (source != me), 1, 0)
        pl.semaphore_wait(barrier, greeted)

        @pl.loop(0, ahead)
        def _(k):
            fetch(k)

        own_part[...] = jnp.zeros_like(own_part)
        key_at = lax.broadcasted_iota(jnp.int32, (span, total_rows), 0)
        for b in range(2):
            low, high = bounds_ref[2 * b : 2 * b + 1, :], bounds_ref[2 * b + 1 : 2 * b + 2, :]
            bias[b] = jnp.where((key_at >= low) & (key_at <= high), 0.0, MASKED)

    @pl.when((g > 0) & (g + ahead - 1 < local_heads))
    def _():
        fetch(g + ahead - 1)

    @pl.when(g > 0)
    def _():
        give(g - 1)

    for n in range(2):
        here, away = row_copies(g, n)
        here.wait()
        away.wait_recv()

    @pl.loop(0, slots)
    def _(j):
        source = base - steps + j
        at = pl.ds(pl.multiple_of(j * tokens, tokens), tokens)

        @pl.when(source < 0)
        def _():
            k_s[at, :] = jnp.zeros((tokens, size_head), k_s.dtype)
            v_s[at, :] = jnp.zeros((tokens, size_head), v_s.dtype)

        @pl.when(source == me)
        def _():
            k_s[at, :] = own_ref[core * local_heads + g, 0]
            v_s[at, :] = own_ref[core * local_heads + g, 1]

        @pl.when((source >= 0) & (source != me))
        def _():
            pltpu.make_async_copy(window.at[g, j], window.at[g, j], kv_recv.at[g, j]).wait()
            k_s[at, :] = window[g, j, 0]
            v_s[at, :] = window[g, j, 1]

    kt_s[...] = k_s[...].T
    vt_s[...] = v_s[...].T
    dk_s[...] = jnp.zeros_like(dk_s)
    dv_s[...] = jnp.zeros_like(dv_s)

    for b in range(2):
        near = pl.ds(b * head_size * tokens, span)

        @pl.loop(0, total_rows // rows)
        def _(c):
            toks = pl.ds(pl.multiple_of(c * part, part), part)
            lanes = pl.ds(pl.multiple_of(c * rows, rows), rows)
            q = q_s[g, b, toks].reshape(rows, size_head)
            do = do_s[g, b, toks].reshape(rows, size_head)
            x = nt(k_s[near, :], q) + bias[b, :, lanes]
            top = jnp.max(x, axis=0, keepdims=True)
            e = jnp.exp((x - top) * score_scale)
            inv = 1.0 / jnp.sum(e, axis=0, keepdims=True)
            p = e * inv
            w = p.astype(jnp.bfloat16)
            ot = nn(vt_s[:, near], w).astype(jnp.bfloat16)
            dot_f = do.T.astype(jnp.float32)
            delta = jnp.sum(dot_f * ot.astype(jnp.float32), axis=0, keepdims=True)
            o_s[g, b, toks] = ot.T.reshape(part, width, size_head)
            dp = nt(v_s[near, :], do)
            ds = (p * (dp - delta)).astype(jnp.bfloat16)
            dv_s[near, :] += nn(w, do)
            dk_s[near, :] += nn(ds, q)
            dqt = (nn(kt_s[:, near], ds) * score_scale).astype(jnp.bfloat16)
            dq_s[g, b, toks] = dqt.T.reshape(part, width, size_head)

    for j in range(slots):
        at = pl.ds(j * tokens, tokens)
        leaving[g, j, 0] = (dk_s[at, :] * score_scale).astype(leaving.dtype)
        leaving[g, j, 1] = dv_s[at, :].astype(leaving.dtype)
    at = pl.ds(pl.multiple_of((steps + core * head_size) * tokens, tokens), tokens)
    own_part[core * local_heads + g, 0] += dk_s[at, :] * score_scale
    own_part[core * local_heads + g, 1] += dv_s[at, :]

    @pl.when(g >= behind)
    def _():
        finish(g - behind)

    @pl.when(g == local_heads - 1)
    def _():
        give(g)

        @pl.loop(0, behind)
        def _(i):
            finish(g - behind + 1 + i)

        @pl.loop(0, local_heads)
        def _(k):
            each_target(lambda i, side, target: block_copy(k, i, side, target).wait_send())
            each_source(lambda j, source: part_copy(k, j, source).wait_send())
            for n in range(2):
                row_copies(k, n)[1].wait_send()
                here, away = out_copies(k, n)
                here.wait()
                away.wait()


def attention(queries, output_gradient, own, bounds, steps, score_scale):
    tokens, heads, size_head = queries.shape
    kv_count = own.shape[0]
    width = heads // kv_count
    local_heads = kv_count // 2
    span = (steps + 1) * tokens
    slots = steps + 1 + lax.axis_size("head")
    reach = slots * tokens
    total_rows = tokens * width
    rows = min(1024, total_rows)
    q4 = queries.reshape(tokens, kv_count, width, size_head)
    do4 = output_gradient.reshape(tokens, kv_count, width, size_head)
    anywhere = pl.BlockSpec(memory_space=pl.ANY)
    row_shape = jax.ShapeDtypeStruct(q4.shape, jnp.bfloat16)
    full = pl.BlockSpec(own.shape, lambda g: (0, 0, 0, 0))
    half = pl.BlockSpec((kv_count, tokens, size_head), lambda g: (0, 0, 0))
    half_shape = jax.ShapeDtypeStruct((kv_count, tokens, size_head), jnp.bfloat16)
    row_buffer = pltpu.VMEM((local_heads, 2, tokens, width, size_head), jnp.bfloat16)
    pair = pltpu.SemaphoreType.DMA((local_heads, 2))
    outs = pl.pallas_call(
        functools.partial(
            attention_kernel,
            steps,
            rows,
            lax.axis_size("ctx"),
            lax.axis_size("head"),
            min(4, local_heads),
            min(2, local_heads - 1),
            score_scale,
        ),
        grid=(local_heads,),
        in_specs=[pl.BlockSpec((4, total_rows), lambda g: (0, 0)), anywhere, anywhere, full],
        out_specs=[anywhere, anywhere, half, half],
        out_shape=[row_shape, row_shape, half_shape, half_shape],
        scratch_shapes=[
            pltpu.VMEM((local_heads, slots) + own.shape[1:], jnp.bfloat16),
            pltpu.VMEM((local_heads, slots) + own.shape[1:], jnp.bfloat16),
            pltpu.VMEM((kv_count, slots) + own.shape[1:], jnp.bfloat16),
            pltpu.VMEM(own.shape, jnp.float32),
            pltpu.VMEM((2, span, total_rows), jnp.float32),
            row_buffer,
            row_buffer,
            row_buffer,
            row_buffer,
            pltpu.VMEM((reach, size_head), jnp.bfloat16),
            pltpu.VMEM((reach, size_head), jnp.bfloat16),
            pltpu.VMEM((size_head, reach), jnp.bfloat16),
            pltpu.VMEM((size_head, reach), jnp.bfloat16),
            pltpu.VMEM((reach, size_head), jnp.float32),
            pltpu.VMEM((reach, size_head), jnp.float32),
            pltpu.SemaphoreType.DMA((local_heads,)),
            pltpu.SemaphoreType.DMA((local_heads, slots)),
            pltpu.SemaphoreType.DMA((local_heads,)),
            pltpu.SemaphoreType.DMA((kv_count, slots)),
            pair,
            pair,
            pair,
            pair,
            pair,
            pair,
        ],
        compiler_params=pltpu.CompilerParams(
            dimension_semantics=("arbitrary",),
            vmem_limit_bytes=60 << 20,
            collective_id=0,
            has_side_effects=True,
        ),
        name="attention",
    )(bounds, q4, do4, own)
    return outs[0].reshape(queries.shape), outs[1].reshape(queries.shape), outs[2], outs[3]


def body(queries, key_heads, head_values, output_gradient, doc_lengths):
    tokens, heads, size_head = queries.shape
    width = heads // key_heads.shape[1]
    steps = (MOST + tokens - 2) // tokens
    ctx, head_size = lax.axis_index("ctx"), lax.axis_size("head")
    chip = (ctx - ctx % 2) * head_size + lax.axis_index("head")
    within = jnp.arange(tokens, dtype=jnp.int32)
    bounds = []
    for b in range(2):
        base = (chip + b * head_size) * tokens
        window_base = base - steps * tokens
        query_pos = base + within
        bounds += [document_starts(doc_lengths, query_pos) - window_base, query_pos - window_base]
    bounds = jnp.repeat(jnp.stack(bounds, 0), width, axis=1)
    own = jnp.transpose(jnp.stack([key_heads, head_values], 0), (2, 0, 1, 3))
    attended, grad_query, grad_keys, grad_values = attention(
        queries, output_gradient, own, bounds, steps, size_head ** (-0.5)
    )
    grad_keys = jnp.transpose(grad_keys, (1, 0, 2))
    grad_values = jnp.transpose(grad_values, (1, 0, 2))
    return attended, grad_query, grad_keys, grad_values


def solution(mesh):
    whole = P(AXES, None, None)
    return jax.shard_map(
        body,
        mesh=mesh,
        in_specs=(whole, whole, whole, whole, P()),
        out_specs=(whole, whole, whole, whole),
        check_vma=False,
    )
```
